32 devices in a mesh: leaf: 8 (over z, x), vec: 4 (over y, core).
Axes of the slice: x: 2, y: 2, z: 4, core: 2. Of those that a mesh axis runs over, the one named last changes fastest.
Arguments:
- vectors: float32 [32, 65536], P('vec', 'leaf'), may hold values from -15 to 15
- coords: float32 [3, 65536], P(None, 'leaf'), may hold values from 0 to 64, as said below
- leaf_basis: float32 [32, 65536], P(None, 'leaf'), may hold values from -0.375 to 0.375
- node_ops: float32 [496, 32, 128], P('leaf'), may hold values from -0.75 to 0.75
- top_ops: float32 [2, 32, 192], replicated, may hold values from -0.75 to 0.75
- near_target: int32 [1280], P('leaf'), may hold values from 0 to 255, as said below
- near_source: int32 [1280], P('leaf'), may hold values from 0 to 255, as said below
- near_count: int32 [8], P('leaf'), may hold values from 64 to 160, as said below
Outputs:
- product: float32 [32, 65536], P('vec', 'leaf')
- gram_matrix: float32 [32, 32], P(None, 'vec')
The draws below stay inside these ranges and needn't reach their ends.
Inputs may be any that keep to these rules, and one draw needn't show every extreme that they name: `near_target`: slots of one index of leaf name target leaves of that index only; each aligned block of 32 slots of an index names each of its leaves once; in the first run every leaf is paired with itself, and in the second run the first leaf of each index is paired with the leaf just below it and the last leaf with the leaf just above it, where those exist. `near_source`: A source leaf lies within 4 leaves of its target leaf; no pair repeats within one index of leaf. The first near_count[d] slots of index d are live, the rest are padding; some index fills all 160 slots. `coords`: point k lies in the box of its leaf l = k // 256: first coordinate from 0.25 l to 0.25 (l + 1), the other two from 0 to 1.
All inputs are finite; a program needn't handle non-finite values.
Results may differ from the reference program's by a relative error of at most 0.0003.
Values sent between devices are 32-bit elements; how exact they have to be, the bound alone decides.
A program may use at most 64 MiB of HBM per device.

```python
import jax
import jax.numpy as jnp
import numpy as np
from jax import lax

PTS = 256
R = 32
NV = 32
LEAF_DEV = 32
NEAR_REACH = 4
NEAR_EXTRA = 4
PAIR_DEV = 160
NODES_DEV = 62
LEAVES = 256
NPOINTS = 65536
TOPLEV = 2
N_LEAF = 8


SLAB = 0.25


def draw_coords(key, part):
    uniform_unit = jax.random.uniform(key, (3, NPOINTS), jnp.float32)
    leaf_pos = (jnp.arange(NPOINTS, dtype=jnp.int32) // PTS).astype(jnp.float32)
    along_rod = (leaf_pos + uniform_unit[0]) * SLAB
    return jnp.stack([along_rod, uniform_unit[1], uniform_unit[2]], axis=0)


def draw_vectors(key, part):
    base_draw = jnp.clip(jax.random.normal(key, (NV, NPOINTS), jnp.float32), -5.0, 5.0)
    rising = 1.0 + 2.0 * jnp.arange(NPOINTS, dtype=jnp.float32) / NPOINTS
    return base_draw * rising[None, :]


def near_lists(key):
    devices_count = LEAVES // LEAF_DEV
    rounds = NEAR_EXTRA + 1
    span_slots = max(1, (NEAR_EXTRA - 1) * LEAF_DEV)
    factors = jax.random.randint(jax.random.fold_in(key, 11), (3, devices_count), 0, span_slots + 1)
    extra_slots = LEAF_DEV + factors[0] * factors[1] * factors[2] // (span_slots * span_slots)
    extra_slots = jnp.minimum(extra_slots, NEAR_EXTRA * LEAF_DEV)
    busiest = jax.random.randint(jax.random.fold_in(key, 12), (), 0, devices_count)
    extra_slots = jnp.where(jnp.arange(devices_count) == busiest, NEAR_EXTRA * LEAF_DEV, extra_slots)
    tally_count = (LEAF_DEV + extra_slots).astype(jnp.int32)
    width_two = 2 * NEAR_REACH
    candidate = jnp.concatenate([jnp.arange(-NEAR_REACH, 0), jnp.arange(1, NEAR_REACH + 1)]).astype(jnp.int32)
    leaf_ids = jnp.arange(LEAVES, dtype=jnp.int32)
    sources = leaf_ids[:, None] + candidate[None, :]
    inside = (sources >= 0) & (sources < LEAVES)
    scores = jax.random.randint(jax.random.fold_in(key, 13), (LEAVES, width_two), 0, 1 << 20) * width_two + jnp.arange(width_two, dtype=jnp.int32)[None, :]
    position = (leaf_ids % LEAF_DEV)[:, None]
    column_ids = jnp.arange(width_two, dtype=jnp.int32)[None, :]
    forced = (position == 0) & (column_ids == NEAR_REACH - 1) | (position == LEAF_DEV - 1) & (column_ids == NEAR_REACH)
    scores = scores - jnp.where(forced, 1 << 25, 0)
    scores = scores + jnp.where(inside, 0, 1 << 27)
    ranking = jnp.argsort(scores, axis=1)
    chosen = jnp.take_along_axis(sources, ranking[:, :NEAR_EXTRA], axis=1)
    per_round = jnp.concatenate([leaf_ids[:, None], chosen], axis=1)
    round_table = per_round.reshape(devices_count, LEAF_DEV, rounds).transpose(0, 2, 1)
    shuffle_scores = jax.random.randint(jax.random.fold_in(key, 14), (devices_count, rounds, LEAF_DEV), 0, 1 << 20) * LEAF_DEV + jnp.arange(LEAF_DEV, dtype=jnp.int32)[None, None, :]
    shuffle = jnp.argsort(shuffle_scores, axis=2).astype(jnp.int32)
    sources_slot = jnp.take_along_axis(round_table, shuffle, axis=2)
    targets = shuffle + (jnp.arange(devices_count, dtype=jnp.int32) * LEAF_DEV)[:, None, None]
    return (targets.reshape(-1).astype(jnp.int32), sources_slot.reshape(-1).astype(jnp.int32), tally_count)


def draw_near_target(key, part):
    return near_lists(key)[0]


def draw_near_source(key, part):
    return near_lists(key)[1]


def draw_near_count(key, part):
    return near_lists(key)[2]


def block_levels(rng, shape, shards, least, high):
    loudness = 1.0
    for dim, parts in shards:
        heights = jax.random.uniform(jax.random.fold_in(jax.random.fold_in(rng, 6), dim), (parts,), jnp.float32, least / len(shards), high / len(shards))
        loudness = loudness * jnp.repeat(jnp.exp(heights), shape[dim] // parts).reshape((-1,) + (1,) * (len(shape) - 1 - dim))
    return loudness


def gaussian(rng, extent, scale, most, split=(), held_as=jnp.bfloat16):
    drawn = jax.random.normal(rng, extent, jnp.float32) * scale
    if len(split) > 0:
        drawn = block_levels(rng, extent, split, -0.22, 0.18) * drawn
    return jnp.clip(drawn, min=-most, max=most).astype(held_as)


def setup_inputs(seed: int = 0) -> dict:
    arg_keys = jax.random.split(jax.random.key(seed), 9)
    vectors = draw_vectors(jax.random.fold_in(arg_keys[8], 71), 0)
    coords = draw_coords(jax.random.fold_in(arg_keys[8], 71), 0)
    leaf_basis = gaussian(arg_keys[2], (R, NPOINTS), PTS ** -0.5, 0.375, ((1, 8),), jnp.float32)
    node_ops = gaussian(arg_keys[3], (N_LEAF * NODES_DEV, R, 4 * R), (2 * R) ** -0.5, 0.75, ((0, 8),), jnp.float32)
    top_ops = gaussian(arg_keys[4], (TOPLEV, R, 6 * R), (2 * R) ** -0.5, 0.75, (), jnp.float32)
    near_target = draw_near_target(jax.random.fold_in(arg_keys[8], 71), 0)
    near_source = draw_near_source(jax.random.fold_in(arg_keys[8], 71), 0)
    near_count = draw_near_count(jax.random.fold_in(arg_keys[8], 71), 0)
    return {"vectors": vectors, "coords": coords, "leaf_basis": leaf_basis, "node_ops": node_ops, "top_ops": top_ops, "near_target": near_target, "near_source": near_source, "near_count": near_count}


EXACT_ARITHMETIC = lax.Precision.HIGHEST
SIGNAL = 0.1
NUGGET = 0.5
LENGTH = 0.35
EVEN_OFFSETS = (-2, 2, 3)
ODD_OFFSETS = (-3, -2, 2)
TOP_OFFSETS = (-3, -2, 2, 3)

def matern(target_pts, source_pts):
    pair_separation = jnp.zeros((target_pts.shape[1], target_pts.shape[2], source_pts.shape[2]), jnp.float32)
    for axis_id in range(3):
        spacing = target_pts[axis_id][:, :, None] - source_pts[axis_id][:, None, :]
        pair_separation = pair_separation + spacing * spacing
    scaled = jnp.sqrt(3.0 * pair_separation) / LENGTH
    return SIGNAL * (1.0 + scaled) * jnp.exp(-scaled)

def take_rows(padded, count_nodes, pad_width):
    parity_ids = np.arange(count_nodes) % 2
    gathered = []
    for slot_index in range(3):
        shift_by = np.where(parity_ids == 0, EVEN_OFFSETS[slot_index], ODD_OFFSETS[slot_index])
        gathered.append(padded[np.arange(count_nodes) + shift_by + pad_width])
    return jnp.stack(gathered, axis=1)

def couple_level(padded, operators, count_nodes, pad_width, rank_size):
    sources = take_rows(padded, count_nodes, pad_width)
    blocks = operators[:, :, :3 * rank_size].reshape(count_nodes, rank_size, 3, rank_size)
    return jnp.einsum('navr,nras->nvs', sources, blocks, precision=EXACT_ARITHMETIC)

def raise_level(incoming_coefficients, operators, rank_size):
    moved = jnp.einsum('nvr,nrs->nvs', incoming_coefficients, operators[:, :, 3 * rank_size:], precision=EXACT_ARITHMETIC)
    return moved[0::2] + moved[1::2]

def lower_level(field_in, operators, rank_size):
    spread = jnp.repeat(field_in, 2, axis=0)
    return jnp.einsum('nvs,nrs->nvr', spread, operators[:, :, 3 * rank_size:], precision=EXACT_ARITHMETIC)

def through(incoming_coefficients, operators, position, rank_size):
    return jnp.einsum('...r,rs->...s', incoming_coefficients, operators[:, position * rank_size:(position + 1) * rank_size], precision=EXACT_ARITHMETIC)

def couple_top(partners, operators, parity, rank_size):
    far_left, near_left, near_right, far_right = partners
    outer = jnp.where(parity == 0, through(far_right, operators, 3, rank_size), through(far_left, operators, 0, rank_size))
    return through(near_left, operators, 1, rank_size) + through(near_right, operators, 2, rank_size) + outer

def raise_pair(left_coef, right_coef, operators, rank_size):
    return through(left_coef, operators, 4, rank_size) + through(right_coef, operators, 5, rank_size)

def lower_top(field_in, operators, parity, rank_size):
    even_part = jnp.einsum('...s,rs->...r', field_in, operators[:, 4 * rank_size:5 * rank_size], precision=EXACT_ARITHMETIC)
    odd_part = jnp.einsum('...s,rs->...r', field_in, operators[:, 5 * rank_size:6 * rank_size], precision=EXACT_ARITHMETIC)
    return jnp.where(parity == 0, even_part, odd_part)

def reference(vectors, coords, leaf_basis, node_ops, top_ops, near_target, near_source, near_count):
    rank_size = leaf_basis.shape[0]
    columns = vectors.shape[0]
    leaves = LEAVES
    per_pairs = PAIR_DEV
    vec_leaf = jnp.concatenate([vectors, coords], axis=0).reshape(columns + 3, leaves, PTS)
    coord_leaf = coords.reshape(3, leaves, PTS)

    def add_device(accumulated_sum, portion):
        target_ids, source_ids, live_count = portion
        live_mask = (jnp.arange(per_pairs) < live_count).astype(jnp.float32)
        source_rows = jnp.take(vec_leaf, source_ids, axis=1)
        target_pts = jnp.take(coord_leaf, target_ids, axis=1)
        kernel = matern(target_pts, source_rows[columns:])
        contribution = jnp.einsum('vbs,bts->bvt', source_rows[:columns], kernel, precision=EXACT_ARITHMETIC) * live_mask[:, None, None]
        return (accumulated_sum.at[target_ids].add(contribution), None)
    initial = jnp.zeros((leaves, columns, PTS), jnp.float32)
    accumulated_sum, unused = lax.scan(add_device, initial, (near_target.reshape(-1, per_pairs), near_source.reshape(-1, per_pairs), near_count))
    near_part = accumulated_sum.transpose(1, 0, 2).reshape(columns, leaves * PTS)
    leaf_basis_matrix = leaf_basis.reshape(rank_size, leaves, PTS)
    current = jnp.einsum('vlp,rlp->lvr', vectors.reshape(columns, leaves, PTS), leaf_basis_matrix, precision=EXACT_ARITHMETIC)
    per_device = node_ops.reshape(N_LEAF, 2 * LEAF_DEV - 2, rank_size, 4 * rank_size)
    level_ops = []
    level_fields = []
    offset_node = 0
    nodes_here = LEAF_DEV
    while nodes_here >= 2:
        ops_here = per_device[:, offset_node:offset_node + nodes_here].reshape(N_LEAF * nodes_here, rank_size, 4 * rank_size)
        padded = jnp.pad(current, ((3, 3), (0, 0), (0, 0)))
        level_fields.append(couple_level(padded, ops_here, current.shape[0], 3, rank_size))
        level_ops.append(ops_here)
        current = raise_level(current, ops_here, rank_size)
        offset_node += nodes_here
        nodes_here //= 2
    top_levels = top_ops.shape[0]
    top_coef = current
    top_fields = []
    for height in range(top_levels):
        nodes_top = top_coef.shape[0]
        padded_top = jnp.pad(top_coef, ((3, 3), (0, 0), (0, 0)))
        partners = tuple((padded_top[3 + offset:3 + offset + nodes_top] for offset in TOP_OFFSETS))
        parity = (jnp.arange(nodes_top) % 2)[:, None, None]
        top_fields.append(couple_top(partners, top_ops[height], parity, rank_size))
        if height + 1 < top_levels:
            top_coef = raise_pair(top_coef[0::2], top_coef[1::2], top_ops[height], rank_size)
    downward = top_fields[top_levels - 1]
    for height in range(top_levels - 2, -1, -1):
        nodes_top = top_fields[height].shape[0]
        parity = (jnp.arange(nodes_top) % 2)[:, None, None]
        downward = top_fields[height] + lower_top(jnp.repeat(downward, 2, axis=0), top_ops[height], parity, rank_size)
    for index_level in range(len(level_fields) - 1, -1, -1):
        downward = level_fields[index_level] + lower_level(downward, level_ops[index_level], rank_size)
    far_part = jnp.einsum('lvr,rlp->vlp', downward, leaf_basis_matrix, precision=EXACT_ARITHMETIC).reshape(columns, leaves * PTS)
    product = near_part + far_part + NUGGET * vectors
    gram_matrix = jnp.dot(vectors, product.T, precision=EXACT_ARITHMETIC) / NPOINTS
    return (product, gram_matrix)
```

```python
import functools

import jax
import jax.numpy as jnp
from jax import lax
from jax.experimental import pallas as pl
from jax.experimental.pallas import tpu as pltpu
from jax.sharding import PartitionSpec as P

PTS = 256
REACH = 4
SIGNAL = 0.1
NUGGET = 0.5
LENGTH = 0.35
SLAB = 0.25
SCALE = 3.0 ** 0.5 / LENGTH
MESH = pl.DeviceIdType.MESH
F32 = jnp.float32
BF16 = jnp.bfloat16
LANES = 128


def halves(x):
    high = x.astype(BF16)
    return high, (x - high.astype(F32)).astype(BF16)


def dot3(a, b, dims):
    ah, al = halves(a)
    bh, bl = halves(b)

    def one(x, y):
        return lax.dot_general(x, y, (dims, ((), ())), preferred_element_type=F32)

    return one(ah, bh) + (one(al, bh) + one(ah, bl))


NN = ((1,), (0,))
NT = ((1,), (1,))


def kernel(cfg, offs, wts, vecs, coords, basis, ops, tops, out, gram, *scr):
    D, V, LD, RK, rounds, toplev = cfg
    cols = vecs.shape[0]
    NC = cols * V
    L = LD // V
    C = L * PTS
    H = REACH * PTS
    PD = LD * PTS
    (win, vhl, crd, bcol, basis_v, ops_v, tops_v, kh, kl, prod, lev, up, roots, fld, gsend, gpart, gall) = scr[:17]
    (s_loc, s_vec, r_vec, s_x, r_x, s_c, r_c, s_e, r_e, s_u, r_u, s_h, r_h, s_r, r_r, s_o, r_o, s_g, r_g, s_q, r_q) = scr[17:]
    d = lax.axis_index("leaf")
    v = lax.axis_index("vec")
    g = d * V + v
    has_left = g > 0
    has_right = g < D * V - 1

    local_levels = []
    n, base, row = L, 0, 0
    while n >= 2:
        local_levels.append((n, base, row))
        base += n + 4
        row += LD // L * n
        n //= 2
    up_levels = []
    n, base = V, 0
    while n >= 2:
        up_levels.append((n, base, row))
        base += n + 4
        row += n
        n //= 2

    own = pl.ds(v * cols, cols)
    chunk = pl.ds(pl.multiple_of(v * C, C), C)
    loads = [
        pltpu.make_async_copy(vecs.at[:, chunk], win.at[own, pl.ds(H, C)], s_loc.at[0]),
        pltpu.make_async_copy(coords.at[:, chunk], crd.at[:, pl.ds(H, C)], s_loc.at[1]),
        pltpu.make_async_copy(basis.at[:, chunk], basis_v, s_loc.at[2]),
        pltpu.make_async_copy(ops, ops_v, s_loc.at[3]),
        pltpu.make_async_copy(tops, tops_v, s_loc.at[4]),
    ]
    for copy in loads:
        copy.start()
    low_from = pl.ds(pl.multiple_of(jnp.maximum(v * C - H, 0), H), H)
    high_from = pl.ds(pl.multiple_of(jnp.minimum(v * C + C, PD - H), H), H)
    low_loads = [
        pltpu.make_async_copy(vecs.at[:, low_from], win.at[own, pl.ds(0, H)], s_loc.at[5]),
        pltpu.make_async_copy(coords.at[:, low_from], crd.at[:, pl.ds(0, H)], s_loc.at[6]),
    ]
    high_loads = [
        pltpu.make_async_copy(vecs.at[:, high_from], win.at[own, pl.ds(H + C, H)], s_loc.at[7]),
        pltpu.make_async_copy(coords.at[:, high_from], crd.at[:, pl.ds(H + C, H)], s_loc.at[8]),
    ]

    @pl.when(v > 0)
    def _():
        for copy in low_loads:
            copy.start()

    @pl.when(v < V - 1)
    def _():
        for copy in high_loads:
            copy.start()

    barrier = pltpu.get_barrier_semaphore()
    for k in range(1, V):
        pl.semaphore_signal(barrier, inc=1, device_id=(d, lax.rem(v + k, V)), device_id_type=MESH)
    for k in range(1, D):
        pl.semaphore_signal(barrier, inc=1, device_id=(lax.rem(d + k, D), v), device_id_type=MESH)

    @pl.when(d > 0)
    def _():
        for k in range(1, V):
            pl.semaphore_signal(barrier, inc=1, device_id=(d - 1, lax.rem(v + k, V)), device_id_type=MESH)

    @pl.when(d < D - 1)
    def _():
        for k in range(1, V):
            pl.semaphore_signal(barrier, inc=1, device_id=(d + 1, lax.rem(v + k, V)), device_id_type=MESH)

    sides = (d > 0).astype(jnp.int32) + (d < D - 1).astype(jnp.int32)
    pl.semaphore_wait(barrier, V - 1 + D - 1 + (V - 1) * sides)

    def remote(src, dst, ss, rs, where):
        return pltpu.make_async_remote_copy(
            src_ref=src, dst_ref=dst, send_sem=ss, recv_sem=rs, device_id=where, device_id_type=MESH
        )

    def vec_copies(t):
        parts = [(0, t * C, H, C)]
        if t > 0:
            parts.append((1, t * C - H, 0, H))
        if t < V - 1:
            parts.append((2, t * C + C, H + C, H))
        return [
            remote(
                vecs.at[:, pl.ds(src, size)],
                win.at[own, pl.ds(dst, size)],
                s_vec.at[k, t],
                r_vec.at[k, v],
                (d, t),
            )
            for k, src, dst, size in parts
        ]

    cross_right = remote(
        vecs.at[:, pl.ds(PD - H, H)], win.at[own, pl.ds(0, H)], s_x.at[0], r_x.at[0, v], (jnp.minimum(d + 1, D - 1), 0)
    )
    cross_left = remote(
        vecs.at[:, pl.ds(0, H)], win.at[own, pl.ds(H + C, H)], s_x.at[1], r_x.at[1, v], (jnp.maximum(d - 1, 0), V - 1)
    )
    crd_right = remote(
        coords.at[:, pl.ds(PD - H, H)], crd.at[:, pl.ds(0, H)], s_c.at[0], r_c.at[0], (jnp.minimum(d + 1, D - 1), 0)
    )
    crd_left = remote(
        coords.at[:, pl.ds(0, H)], crd.at[:, pl.ds(H + C, H)], s_c.at[1], r_c.at[1], (jnp.maximum(d - 1, 0), V - 1)
    )
    for t in range(V):

        @pl.when(v != t)
        def _(t=t):
            for copy in vec_copies(t):
                copy.start()

    @pl.when(d < D - 1)
    def _():
        cross_right.start()

        @pl.when(v == V - 1)
        def _():
            crd_right.start()

    @pl.when(d > 0)
    def _():
        cross_left.start()

        @pl.when(v == 0)
        def _():
            crd_left.start()

    def zero_nodes(ref, lo, size):
        ref[lo : lo + size] = jnp.zeros((size,) + ref.shape[1:], F32)

    @pl.when(jnp.logical_not(has_left))
    def _():
        win[:, 0:H] = jnp.zeros((NC, H), F32)
        crd[:, 0:H] = jnp.zeros((crd.shape[0], H), F32)
        for n, base, row in local_levels:
            zero_nodes(lev, base, 2)

    @pl.when(jnp.logical_not(has_right))
    def _():
        win[:, H + C :] = jnp.zeros((NC, H), F32)
        crd[:, H + C :] = jnp.zeros((crd.shape[0], H), F32)
        for n, base, row in local_levels:
            zero_nodes(lev, base + 2 + n, 2)

    @pl.when(d == 0)
    def _():
        for n, base, row in up_levels:
            zero_nodes(up, base, 2)

    @pl.when(d == D - 1)
    def _():
        for n, base, row in up_levels:
            zero_nodes(up, base + 2 + n, 2)

    root_base = []
    base = 0
    for k in range(toplev):
        size = D >> k
        zero_nodes(roots, base, 3)
        zero_nodes(roots, base + 3 + size, 3)
        root_base.append(base)
        base += size + 6

    def arrived(dst, rs):
        return pltpu.make_async_copy(dst, dst, rs)

    for copy in loads:
        copy.wait()

    @pl.when(v > 0)
    def _():
        for copy in low_loads:
            copy.wait()

    @pl.when(v < V - 1)
    def _():
        for copy in high_loads:
            copy.wait()

    for s in range(V):
        rows = pl.ds(s * cols, cols)

        @pl.when(v != s)
        def _(s=s, rows=rows):
            arrived(win.at[rows, pl.ds(H, C)], r_vec.at[0, s]).wait()

    def op(i):
        return ops_v[i]

    def coef(ref, i):
        return ref[i][:, :RK]

    def raised(ref, i, row):
        both = dot3(coef(ref, i), op(row), NN) + dot3(coef(ref, i + 1), op(row + 1), NN)
        return pltpu.roll(both, RK, 1)

    for l in range(L):
        points = slice(l * PTS, (l + 1) * PTS)
        lev[2 + l, :, :RK] = dot3(win[:, H + l * PTS : H + (l + 1) * PTS], basis_v[:, points], NT)
    for index, (n, base, row) in enumerate(local_levels):
        for q in range(n // 2):
            value = raised(lev, base + 2 + 2 * q, row + v * n + 2 * q)
            if index + 1 < len(local_levels):
                lev[local_levels[index + 1][1] + 2 + q] = value
            else:
                up[2 + v] = value

    def edge_copies(side, where):
        copies = []
        for k, (n, base, row) in enumerate(local_levels):
            src = base + 2 if side == 0 else base + n
            dst = base + 2 + n if side == 0 else base
            copies.append(
                remote(lev.at[pl.ds(src, 2)], lev.at[pl.ds(dst, 2)], s_e.at[side, k], r_e.at[side, k], where)
            )
        return copies

    left_id = (jnp.maximum(g - 1, 0) // V, lax.rem(jnp.maximum(g - 1, 0), V))
    right_id = (jnp.minimum(g + 1, D * V - 1) // V, lax.rem(jnp.minimum(g + 1, D * V - 1), V))
    edges_left = edge_copies(0, left_id)
    edges_right = edge_copies(1, right_id)

    @pl.when(has_left)
    def _():
        for copy in edges_left:
            copy.start()

    @pl.when(has_right)
    def _():
        for copy in edges_right:
            copy.start()

    up_copies = [
        remote(up.at[2 + v], up.at[2 + v], s_u.at[k], r_u.at[v], (d, lax.rem(v + k, V))) for k in range(1, V)
    ]
    for copy in up_copies:
        copy.start()

    for s in range(V):
        rows = pl.ds(s * cols, cols)

        @pl.when(jnp.logical_and(v > 0, v != s))
        def _(s=s, rows=rows):
            arrived(win.at[rows, pl.ds(0, H)], r_vec.at[1, s]).wait()

        @pl.when(jnp.logical_and(v < V - 1, v != s))
        def _(s=s, rows=rows):
            arrived(win.at[rows, pl.ds(H + C, H)], r_vec.at[2, s]).wait()

        @pl.when(jnp.logical_and(v == 0, d > 0))
        def _(s=s, rows=rows):
            arrived(win.at[rows, pl.ds(0, H)], r_x.at[0, s]).wait()

        @pl.when(jnp.logical_and(v == V - 1, d < D - 1))
        def _(s=s, rows=rows):
            arrived(win.at[rows, pl.ds(H + C, H)], r_x.at[1, s]).wait()

    @pl.when(jnp.logical_and(v == 0, d > 0))
    def _():
        arrived(crd.at[:, pl.ds(0, H)], r_c.at[0]).wait()

    @pl.when(jnp.logical_and(v == V - 1, d < D - 1))
    def _():
        arrived(crd.at[:, pl.ds(H + C, H)], r_c.at[1]).wait()

    origin = (g * L).astype(F32) * SLAB
    first = lax.broadcasted_iota(jnp.int32, crd.shape, 0) == 0
    crd[...] = (crd[...] - jnp.where(first, origin, 0.0)) * SCALE

    def spread(i, carry):
        at = pl.ds(pl.multiple_of(i * LANES, LANES), LANES)
        tall = crd[:, at].T
        for axis in range(3):
            bcol[i // 2, axis, pl.ds(pl.multiple_of(lax.rem(i, 2) * LANES, LANES), LANES), :] = jnp.broadcast_to(
                tall[:, axis : axis + 1], (LANES, LANES)
            )
        return carry

    lax.fori_loop(0, (C + 2 * H) // LANES, spread, 0)

    for leaf in range(L + 2 * REACH):
        high, low = halves(win[:, leaf * PTS : (leaf + 1) * PTS])
        vhl[leaf, :NC] = high
        vhl[leaf, NC:] = low

    step = 64

    def near(t, carry):
        here = pl.ds(pl.multiple_of(H + t * PTS, PTS), PTS)
        target = [crd[axis : axis + 1, here] for axis in range(3)]
        total = jnp.zeros((NC, PTS), F32)
        for r in range(rounds):
            slot = r * LD + v * L + t
            source = bcol[offs[slot]]
            for sub in range(PTS // step):
                rows = slice(sub * step, (sub + 1) * step)
                for half in range(PTS // LANES):
                    lanes = slice(half * LANES, (half + 1) * LANES)
                    dist = None
                    for axis in range(3):
                        gap = source[axis, rows] - target[axis][:, lanes]
                        dist = gap * gap if dist is None else dist + gap * gap
                    u = dist * lax.rsqrt(jnp.maximum(dist, 1e-30))
                    block = (1.0 + u) * jnp.exp(-u)
                    high, low = halves(block)
                    kh[r, rows, lanes] = high
                    kl[r, rows, lanes] = low
            moved = vhl[offs[slot]]
            both = jnp.dot(moved, kh[r], preferred_element_type=F32)
            small = jnp.dot(moved[:NC], kl[r], preferred_element_type=F32)
            total = total + ((both[:NC] + both[NC:]) + small) * wts[slot]
        prod[:, pl.ds(pl.multiple_of(t * PTS, PTS), PTS)] = total
        return carry

    cut = L // 2
    lax.fori_loop(0, cut, near, 0)

    for s in range(V):

        @pl.when(v != s)
        def _(s=s):
            arrived(up.at[2 + s], r_u.at[s]).wait()

    for copy in up_copies:
        copy.wait_send()
    for index, (n, base, row) in enumerate(up_levels):
        for q in range(n // 2):
            value = raised(up, base + 2 + 2 * q, row + 2 * q)
            if index + 1 < len(up_levels):
                up[up_levels[index + 1][1] + 2 + q] = value
            else:
                roots[3 + d] = value

    def halo_copies(side, where):
        copies = []
        for k, (n, base, row) in enumerate(up_levels):
            src = base + 2 if side == 0 else base + n
            dst = base + 2 + n if side == 0 else base
            copies.append(
                remote(up.at[pl.ds(src, 2)], up.at[pl.ds(dst, 2)], s_h.at[side, k], r_h.at[side, k], where)
            )
        return copies

    halos_left = halo_copies(0, (jnp.maximum(d - 1, 0), v))
    halos_right = halo_copies(1, (jnp.minimum(d + 1, D - 1), v))

    @pl.when(d > 0)
    def _():
        for copy in halos_left:
            copy.start()

    @pl.when(d < D - 1)
    def _():
        for copy in halos_right:
            copy.start()

    root_copies = [
        remote(roots.at[3 + d], roots.at[3 + d], s_r.at[k], r_r.at[d], (lax.rem(d + k, D), v)) for k in range(1, D)
    ]
    for copy in root_copies:
        copy.start()

    lax.fori_loop(cut, L, near, 0)

    for s in range(D):

        @pl.when(d != s)
        def _(s=s):
            arrived(roots.at[3 + s], r_r.at[s]).wait()

    for copy in root_copies:
        copy.wait_send()

    @pl.when(d > 0)
    def _():
        for copy in halos_left:
            copy.wait_send()
        for k, (n, base, row) in enumerate(up_levels):
            arrived(up.at[pl.ds(base, 2)], r_h.at[1, k]).wait()

    @pl.when(d < D - 1)
    def _():
        for copy in halos_right:
            copy.wait_send()
        for k, (n, base, row) in enumerate(up_levels):
            arrived(up.at[pl.ds(base + 2 + n, 2)], r_h.at[0, k]).wait()

    @pl.when(has_left)
    def _():
        for copy in edges_left:
            copy.wait_send()
        for k, (n, base, row) in enumerate(local_levels):
            arrived(lev.at[pl.ds(base, 2)], r_e.at[1, k]).wait()

    @pl.when(has_right)
    def _():
        for copy in edges_right:
            copy.wait_send()
        for k, (n, base, row) in enumerate(local_levels):
            arrived(lev.at[pl.ds(base + 2 + n, 2)], r_e.at[0, k]).wait()

    top_fields = []
    for k in range(toplev):
        base, size = root_base[k], D >> k
        node = d // (1 << k)
        odd = lax.rem(node, 2).astype(F32)
        weights = (odd, 1.0, 1.0, 1.0 - odd)
        table = tops_v[k]
        partners = jnp.concatenate([coef(roots, base + 3 + node + o) for o in (-3, -2, 2, 3)], axis=0)
        moved = dot3(partners, table[:, : 4 * RK], NN)
        total = moved[:RK * 0 + NC] * weights[0]
        for j in range(1, 4):
            total = total + pltpu.roll(moved[j * NC : (j + 1) * NC], LANES - j * RK, 1) * weights[j]
        top_fields.append(total[:, :RK])
        if k + 1 < toplev:
            for q in range(size // 2):
                value = dot3(coef(roots, base + 3 + 2 * q), table[:, 4 * RK : 5 * RK], NN) + dot3(
                    coef(roots, base + 4 + 2 * q), table[:, 5 * RK :], NN
                )
                roots[root_base[k + 1] + 3 + q, :, :RK] = value
    down = top_fields[toplev - 1]
    for k in range(toplev - 2, -1, -1):
        odd = lax.rem(d // (1 << k), 2).astype(F32)
        table = tops_v[k]
        even_part = dot3(down, table[:, 4 * RK : 5 * RK], NT)
        odd_part = dot3(down, table[:, 5 * RK :], NT)
        down = top_fields[k] + even_part * (1.0 - odd) + odd_part * odd

    def coupled(ref, sources, row):
        moved = dot3(jnp.concatenate([coef(ref, i) for i in sources], axis=0), op(row), NN)
        return (
            moved[:NC]
            + pltpu.roll(moved[NC : 2 * NC], LANES - RK, 1)
            + pltpu.roll(moved[2 * NC :], LANES - 2 * RK, 1)
        )[:, :RK]

    def lowered(parent, row):
        zeros = jnp.zeros((NC, 3 * RK), F32)
        return dot3(jnp.concatenate([zeros, parent], axis=1), op(row), NT)

    for index in range(len(up_levels) - 1, -1, -1):
        n, base, row = up_levels[index]
        node = v // (V // n)
        odd = lax.rem(node, 2)
        at = base + 2 + node
        sources = (at - 2 - odd, at + 2 - 4 * odd, at + 3 - odd)
        down = coupled(up, sources, row + node) + lowered(down, row + node)
    downs = [down]
    for index in range(len(local_levels) - 1, -1, -1):
        n, base, row = local_levels[index]
        fresh = []
        for i in range(n):
            shifts = (-2, 2, 3) if i % 2 == 0 else (-3, -2, 2)
            sources = [base + 2 + i + o for o in shifts]
            where = row + v * n + i
            fresh.append(coupled(lev, sources, where) + lowered(downs[i // 2], where))
        downs = fresh

    inner = jnp.zeros((NC, NC), F32)
    for l in range(L):
        points = slice(l * PTS, (l + 1) * PTS)
        mine = win[:, H + l * PTS : H + (l + 1) * PTS]
        value = prod[:, points] + dot3(downs[l], basis_v[:, points], NN) + NUGGET * mine
        prod[:, points] = value
        inner = inner + dot3(value, mine, NT)
    for t in range(V):
        gsend[t, :, :NC] = inner[t * cols : (t + 1) * cols]

    def home(t):
        return remote(
            prod.at[pl.ds(t * cols, cols), :], out.at[:, chunk], s_o.at[t], r_o.at[v], (d, t)
        )

    def inner_copy(t):
        return remote(gsend.at[t], gpart.at[v], s_g.at[t], r_g.at[v], (d, t))

    for t in range(V):

        @pl.when(v != t)
        def _(t=t):
            inner_copy(t).start()

    stay = pltpu.make_async_copy(prod.at[own, :], out.at[:, chunk], s_loc.at[9])
    stay.start()
    for t in range(V):

        @pl.when(v != t)
        def _(t=t):
            home(t).start()

    gpart[v] = gsend[v]
    for s in range(V):

        @pl.when(v != s)
        def _(s=s):
            arrived(gpart.at[s], r_g.at[s]).wait()

    group = gpart[0]
    for s in range(1, V):
        group = group + gpart[s]
    gall[d] = group
    group_copies = [
        remote(gall.at[d], gall.at[d], s_q.at[k], r_q.at[d], (lax.rem(d + k, D), v)) for k in range(1, D)
    ]
    for copy in group_copies:
        copy.start()
    stay.wait()

    for t in range(V):

        @pl.when(v != t)
        def _(t=t):
            for copy in vec_copies(t):
                copy.wait_send()
            home(t).wait_send()
            inner_copy(t).wait_send()
            arrived(out.at[:, pl.ds(t * C, C)], r_o.at[t]).wait()

    @pl.when(d < D - 1)
    def _():
        cross_right.wait_send()

        @pl.when(v == V - 1)
        def _():
            crd_right.wait_send()

    @pl.when(d > 0)
    def _():
        cross_left.wait_send()

        @pl.when(v == 0)
        def _():
            crd_left.wait_send()

    for s in range(D):

        @pl.when(d != s)
        def _(s=s):
            arrived(gall.at[s], r_q.at[s]).wait()

    for copy in group_copies:
        copy.wait_send()
    whole = gall[0]
    for s in range(1, D):
        whole = whole + gall[s]
    gram[...] = whole * (1.0 / (D * PD))


def on_device(D, V, vectors, coords, leaf_basis, node_ops, top_ops, near_target, near_source, near_count):
    cols, points = vectors.shape
    rank = leaf_basis.shape[0]
    LD = points // PTS
    L = LD // V
    NC = cols * V
    C, H = L * PTS, REACH * PTS
    slots = near_target.shape[0]
    rounds = slots // LD
    toplev = top_ops.shape[0]
    base_leaf = lax.axis_index("leaf") * LD
    live = (jnp.arange(slots, dtype=jnp.int32) < near_count[0]).reshape(rounds, LD, 1)
    local = (near_target - base_leaf).reshape(rounds, LD, 1)
    shift = (near_source - near_target).reshape(rounds, LD, 1)
    hit = (local == jnp.arange(LD, dtype=jnp.int32)) & live
    offs = jnp.sum(jnp.where(hit, shift, 0), axis=1) + jnp.arange(LD, dtype=jnp.int32) % L + REACH
    offs = jnp.clip(offs, 0, L + 2 * REACH - 1).reshape(-1)
    wts = jnp.sum(jnp.where(hit, SIGNAL, 0.0).astype(F32), axis=1).reshape(-1)
    coords8 = jnp.pad(coords, ((0, 5), (0, 0)))

    def total(n):
        size = 0
        while n >= 2:
            size += n + 4
            n //= 2
        return size

    def depth(n):
        return max(1, n.bit_length() - 1)

    root_nodes = sum((D >> k) + 6 for k in range(toplev))
    dma = pltpu.SemaphoreType.DMA
    vmem = pltpu.VMEM
    scratch = [
        vmem((NC, C + 2 * H), F32),
        vmem((L + 2 * REACH, 2 * NC, PTS), BF16),
        vmem((8, C + 2 * H), F32),
        vmem((L + 2 * REACH, 3, PTS, LANES), F32),
        vmem((rank, C), F32),
        vmem(node_ops.shape, F32),
        vmem(top_ops.shape, F32),
        vmem((rounds, PTS, PTS), BF16),
        vmem((rounds, PTS, PTS), BF16),
        vmem((NC, C), F32),
        vmem((total(L), NC, LANES), F32),
        vmem((total(V), NC, LANES), F32),
        vmem((root_nodes, NC, LANES), F32),
        vmem((8, LANES), F32),
        vmem((V, cols, LANES), F32),
        vmem((V, cols, LANES), F32),
        vmem((D, cols, LANES), F32),
        dma((10,)),
        dma((3, V)),
        dma((3, V)),
        dma((2,)),
        dma((2, V)),
        dma((2,)),
        dma((2,)),
        dma((2, depth(L))),
        dma((2, depth(L))),
        dma((V,)),
        dma((V,)),
        dma((2, depth(V))),
        dma((2, depth(V))),
        dma((D,)),
        dma((D,)),
        dma((V,)),
        dma((V,)),
        dma((V,)),
        dma((V,)),
        dma((D,)),
        dma((D,)),
    ]
    smem = pl.BlockSpec(memory_space=pltpu.SMEM)
    anyw = pl.BlockSpec(memory_space=pl.ANY)
    product, gram = pl.pallas_call(
        functools.partial(kernel, (D, V, LD, rank, rounds, toplev)),
        out_shape=(
            jax.ShapeDtypeStruct((cols, points), F32),
            jax.ShapeDtypeStruct((cols, LANES), F32),
        ),
        in_specs=[smem, smem, anyw, anyw, anyw, anyw, anyw],
        out_specs=(anyw, pl.BlockSpec(memory_space=pltpu.VMEM)),
        scratch_shapes=scratch,
        compiler_params=pltpu.CompilerParams(
            collective_id=0, has_side_effects=True, vmem_limit_bytes=40 << 20
        ),
        name="hmatrix",
    )(offs, wts, vectors, coords8, leaf_basis, node_ops, top_ops)
    return product, gram[:, :NC].T


def solution(mesh):
    return jax.shard_map(
        functools.partial(on_device, mesh.shape["leaf"], mesh.shape["vec"]),
        mesh=mesh,
        in_specs=(
            P("vec", "leaf"),
            P(None, "leaf"),
            P(None, "leaf"),
            P("leaf", None, None),
            P(),
            P("leaf"),
            P("leaf"),
            P("leaf"),
        ),
        out_specs=(P("vec", "leaf"), P(None, "vec")),
        check_vma=False,
    )
```

```python
import functools

import jax
import jax.numpy as jnp
from jax import lax
from jax.experimental import pallas as pl
from jax.experimental.pallas import tpu as pltpu
from jax.sharding import PartitionSpec as P

PTS = 256
REACH = 4
SIGNAL = 0.1
NUGGET = 0.5
LENGTH = 0.35
SLAB = 0.25
SCALE = 3.0 ** 0.5 / LENGTH
MESH = pl.DeviceIdType.MESH
F32 = jnp.float32
BF16 = jnp.bfloat16
LANES = 128


def halves(x):
    high = x.astype(BF16)
    return high, (x - high.astype(F32)).astype(BF16)


def dot3(a, b, dims):
    ah, al = halves(a)
    bh, bl = halves(b)

    def one(x, y):
        return lax.dot_general(x, y, (dims, ((), ())), preferred_element_type=F32)

    return one(ah, bh) + (one(al, bh) + one(ah, bl))


NN = ((1,), (0,))
NT = ((1,), (1,))


def kernel(cfg, offs, wts, vecs, coords, basis, ops, tops, out, gram, *scr):
    D, V, LD, RK, rounds, toplev = cfg
    cols = vecs.shape[0]
    NC = cols * V
    L = LD // V
    C = L * PTS
    H = REACH * PTS
    PD = LD * PTS
    (win, vhl, crd, bcol, basis_v, ops_v, tops_v, kh, kl, prod, lev, up, roots, fld, gsend, gpart, gall) = scr[:17]
    (s_loc, s_vec, r_vec, s_x, r_x, s_c, r_c, s_e, r_e, s_u, r_u, s_h, r_h, s_r, r_r, s_o, r_o, s_g, r_g, s_q, r_q) = scr[17:]
    d = lax.axis_index("leaf")
    v = lax.axis_index("vec")
    g = d * V + v
    has_left = g > 0
    has_right = g < D * V - 1

    local_levels = []
    n, base, row = L, 0, 0
    while n >= 2:
        local_levels.append((n, base, row))
        base += n + 4
        row += LD // L * n
        n //= 2
    up_levels = []
    n, base = V, 0
    while n >= 2:
        up_levels.append((n, base, row))
        base += n + 4
        row += n
        n //= 2

    own = pl.ds(v * cols, cols)
    chunk = pl.ds(pl.multiple_of(v * C, C), C)
    loads = [
        pltpu.make_async_copy(vecs.at[:, chunk], win.at[own, pl.ds(H, C)], s_loc.at[0]),
        pltpu.make_async_copy(coords.at[:, chunk], crd.at[:, pl.ds(H, C)], s_loc.at[1]),
        pltpu.make_async_copy(basis.at[:, chunk], basis_v, s_loc.at[2]),
        pltpu.make_async_copy(ops, ops_v, s_loc.at[3]),
        pltpu.make_async_copy(tops, tops_v, s_loc.at[4]),
    ]
    for copy in loads:
        copy.start()
    low_from = pl.ds(pl.multiple_of(jnp.maximum(v * C - H, 0), H), H)
    high_from = pl.ds(pl.multiple_of(jnp.minimum(v * C + C, PD - H), H), H)
    low_loads = [
        pltpu.make_async_copy(vecs.at[:, low_from], win.at[own, pl.ds(0, H)], s_loc.at[5]),
        pltpu.make_async_copy(coords.at[:, low_from], crd.at[:, pl.ds(0, H)], s_loc.at[6]),
    ]
    high_loads = [
        pltpu.make_async_copy(vecs.at[:, high_from], win.at[own, pl.ds(H + C, H)], s_loc.at[7]),
        pltpu.make_async_copy(coords.at[:, high_from], crd.at[:, pl.ds(H + C, H)], s_loc.at[8]),
    ]

    @pl.when(v > 0)
    def _():
        for copy in low_loads:
            copy.start()

    @pl.when(v < V - 1)
    def _():
        for copy in high_loads:
            copy.start()

    barrier = pltpu.get_barrier_semaphore()
    for k in range(1, V):
        pl.semaphore_signal(barrier, inc=1, device_id=(d, lax.rem(v + k, V)), device_id_type=MESH)
    for k in range(1, D):
        pl.semaphore_signal(barrier, inc=1, device_id=(lax.rem(d + k, D), v), device_id_type=MESH)

    @pl.when(d > 0)
    def _():
        for k in range(1, V):
            pl.semaphore_signal(barrier, inc=1, device_id=(d - 1, lax.rem(v + k, V)), device_id_type=MESH)

    @pl.when(d < D - 1)
    def _():
        for k in range(1, V):
            pl.semaphore_signal(barrier, inc=1, device_id=(d + 1, lax.rem(v + k, V)), device_id_type=MESH)

    sides = (d > 0).astype(jnp.int32) + (d < D - 1).astype(jnp.int32)
    pl.semaphore_wait(barrier, V - 1 + D - 1 + (V - 1) * sides)

    def remote(src, dst, ss, rs, where):
        return pltpu.make_async_remote_copy(
            src_ref=src, dst_ref=dst, send_sem=ss, recv_sem=rs, device_id=where, device_id_type=MESH
        )

    def vec_copies(t):
        parts = [(0, t * C, H, C)]
        if t > 0:
            parts.append((1, t * C - H, 0, H))
        if t < V - 1:
            parts.append((2, t * C + C, H + C, H))
        return [
            remote(
                vecs.at[:, pl.ds(src, size)],
                win.at[own, pl.ds(dst, size)],
                s_vec.at[k, t],
                r_vec.at[k, v],
                (d, t),
            )
            for k, src, dst, size in parts
        ]

    cross_right = remote(
        vecs.at[:, pl.ds(PD - H, H)], win.at[own, pl.ds(0, H)], s_x.at[0], r_x.at[0, v], (jnp.minimum(d + 1, D - 1), 0)
    )
    cross_left = remote(
        vecs.at[:, pl.ds(0, H)], win.at[own, pl.ds(H + C, H)], s_x.at[1], r_x.at[1, v], (jnp.maximum(d - 1, 0), V - 1)
    )
    crd_right = remote(
        coords.at[:, pl.ds(PD - H, H)], crd.at[:, pl.ds(0, H)], s_c.at[0], r_c.at[0], (jnp.minimum(d + 1, D - 1), 0)
    )
    crd_left = remote(
        coords.at[:, pl.ds(0, H)], crd.at[:, pl.ds(H + C, H)], s_c.at[1], r_c.at[1], (jnp.maximum(d - 1, 0), V - 1)
    )
    for t in range(V):

        @pl.when(v != t)
        def _(t=t):
            for copy in vec_copies(t):
                copy.start()

    @pl.when(d < D - 1)
    def _():
        cross_right.start()

        @pl.when(v == V - 1)
        def _():
            crd_right.start()

    @pl.when(d > 0)
    def _():
        cross_left.start()

        @pl.when(v == 0)
        def _():
            crd_left.start()

    def zero_nodes(ref, lo, size):
        ref[lo : lo + size] = jnp.zeros((size,) + ref.shape[1:], F32)

    @pl.when(jnp.logical_not(has_left))
    def _():
        win[:, 0:H] = jnp.zeros((NC, H), F32)
        crd[:, 0:H] = jnp.zeros((crd.shape[0], H), F32)
        for n, base, row in local_levels:
            zero_nodes(lev, base, 2)

    @pl.when(jnp.logical_not(has_right))
    def _():
        win[:, H + C :] = jnp.zeros((NC, H), F32)
        crd[:, H + C :] = jnp.zeros((crd.shape[0], H), F32)
        for n, base, row in local_levels:
            zero_nodes(lev, base + 2 + n, 2)

    @pl.when(d == 0)
    def _():
        for n, base, row in up_levels:
            zero_nodes(up, base, 2)

    @pl.when(d == D - 1)
    def _():
        for n, base, row in up_levels:
            zero_nodes(up, base + 2 + n, 2)

    root_base = []
    base = 0
    for k in range(toplev):
        size = D >> k
        zero_nodes(roots, base, 3)
        zero_nodes(roots, base + 3 + size, 3)
        root_base.append(base)
        base += size + 6

    def arrived(dst, rs):
        return pltpu.make_async_copy(dst, dst, rs)

    for copy in loads:
        copy.wait()

    @pl.when(v > 0)
    def _():
        for copy in low_loads:
            copy.wait()

    @pl.when(v < V - 1)
    def _():
        for copy in high_loads:
            copy.wait()

    origin = (g * L).astype(F32) * SLAB

    def scale_points(lo, size):
        points = crd[:, lo : lo + size]
        first = lax.broadcasted_iota(jnp.int32, points.shape, 0) == 0
        crd[:, lo : lo + size] = (points - jnp.where(first, origin, 0.0)) * SCALE

    def spread_leaves(lo, count):
        pack = 4

        def spread(i, carry):
            for j in range(pack):
                leaf = lo + i * pack + j
                for half in range(PTS // LANES):
                    at = pl.ds(pl.multiple_of(leaf * PTS + half * LANES, LANES), LANES)
                    tall = crd[:, at].T
                    for axis in range(3):
                        bcol[leaf, axis, half * LANES : (half + 1) * LANES, :] = jnp.broadcast_to(
                            tall[:, axis : axis + 1], (LANES, LANES)
                        )
            return carry

        lax.fori_loop(0, count // pack, spread, 0)

    scale_points(H, C)
    spread_leaves(REACH, L)

    for s in range(V):
        rows = pl.ds(s * cols, cols)

        @pl.when(v != s)
        def _(s=s, rows=rows):
            arrived(win.at[rows, pl.ds(H, C)], r_vec.at[0, s]).wait()

    def op(i):
        return ops_v[i]

    def coef(ref, i):
        return ref[i][:, :RK]

    def raised(ref, i, row):
        both = dot3(coef(ref, i), op(row), NN) + dot3(coef(ref, i + 1), op(row + 1), NN)
        return pltpu.roll(both, RK, 1)

    for l in range(L):
        points = slice(l * PTS, (l + 1) * PTS)
        lev[2 + l, :, :RK] = dot3(win[:, H + l * PTS : H + (l + 1) * PTS], basis_v[:, points], NT)
    for index, (n, base, row) in enumerate(local_levels):
        for q in range(n // 2):
            value = raised(lev, base + 2 + 2 * q, row + v * n + 2 * q)
            if index + 1 < len(local_levels):
                lev[local_levels[index + 1][1] + 2 + q] = value
            else:
                up[2 + v] = value

    def edge_copies(side, where):
        copies = []
        for k, (n, base, row) in enumerate(local_levels):
            src = base + 2 if side == 0 else base + n
            dst = base + 2 + n if side == 0 else base
            copies.append(
                remote(lev.at[pl.ds(src, 2)], lev.at[pl.ds(dst, 2)], s_e.at[side, k], r_e.at[side, k], where)
            )
        return copies

    left_id = (jnp.maximum(g - 1, 0) // V, lax.rem(jnp.maximum(g - 1, 0), V))
    right_id = (jnp.minimum(g + 1, D * V - 1) // V, lax.rem(jnp.minimum(g + 1, D * V - 1), V))
    edges_left = edge_copies(0, left_id)
    edges_right = edge_copies(1, right_id)

    @pl.when(has_left)
    def _():
        for copy in edges_left:
            copy.start()

    @pl.when(has_right)
    def _():
        for copy in edges_right:
            copy.start()

    up_copies = [
        remote(up.at[2 + v], up.at[2 + v], s_u.at[k], r_u.at[v], (d, lax.rem(v + k, V))) for k in range(1, V)
    ]
    for copy in up_copies:
        copy.start()

    for s in range(V):
        rows = pl.ds(s * cols, cols)

        @pl.when(jnp.logical_and(v > 0, v != s))
        def _(s=s, rows=rows):
            arrived(win.at[rows, pl.ds(0, H)], r_vec.at[1, s]).wait()

        @pl.when(jnp.logical_and(v < V - 1, v != s))
        def _(s=s, rows=rows):
            arrived(win.at[rows, pl.ds(H + C, H)], r_vec.at[2, s]).wait()

        @pl.when(jnp.logical_and(v == 0, d > 0))
        def _(s=s, rows=rows):
            arrived(win.at[rows, pl.ds(0, H)], r_x.at[0, s]).wait()

        @pl.when(jnp.logical_and(v == V - 1, d < D - 1))
        def _(s=s, rows=rows):
            arrived(win.at[rows, pl.ds(H + C, H)], r_x.at[1, s]).wait()

    @pl.when(jnp.logical_and(v == 0, d > 0))
    def _():
        arrived(crd.at[:, pl.ds(0, H)], r_c.at[0]).wait()

    @pl.when(jnp.logical_and(v == V - 1, d < D - 1))
    def _():
        arrived(crd.at[:, pl.ds(H + C, H)], r_c.at[1]).wait()

    scale_points(0, H)
    scale_points(H + C, H)
    spread_leaves(0, REACH)
    spread_leaves(REACH + L, REACH)

    for leaf in range(L + 2 * REACH):
        high, low = halves(win[:, leaf * PTS : (leaf + 1) * PTS])
        vhl[leaf, :NC] = high
        vhl[leaf, NC:] = low

    step = 64

    def near(t, carry):
        here = pl.ds(pl.multiple_of(H + t * PTS, PTS), PTS)
        target = [crd[axis : axis + 1, here] for axis in range(3)]
        total = jnp.zeros((NC, PTS), F32)
        for r in range(rounds):
            slot = r * LD + v * L + t
            source = bcol[offs[slot]]
            for sub in range(PTS // step):
                rows = slice(sub * step, (sub + 1) * step)
                for half in range(PTS // LANES):
                    lanes = slice(half * LANES, (half + 1) * LANES)
                    dist = None
                    for axis in range(3):
                        gap = source[axis, rows] - target[axis][:, lanes]
                        dist = gap * gap if dist is None else dist + gap * gap
                    u = dist * lax.rsqrt(jnp.maximum(dist, 1e-30))
                    block = (1.0 + u) * jnp.exp(-u)
                    high, low = halves(block)
                    kh[r, rows, lanes] = high
                    kl[r, rows, lanes] = low
            moved = vhl[offs[slot]]
            both = jnp.dot(moved, kh[r], preferred_element_type=F32)
            small = jnp.dot(moved[:NC], kl[r], preferred_element_type=F32)
            total = total + ((both[:NC] + both[NC:]) + small) * wts[slot]
        prod[:, pl.ds(pl.multiple_of(t * PTS, PTS), PTS)] = total
        return carry

    cut = L // 2
    lax.fori_loop(0, cut, near, 0)

    for s in range(V):

        @pl.when(v != s)
        def _(s=s):
            arrived(up.at[2 + s], r_u.at[s]).wait()

    for copy in up_copies:
        copy.wait_send()
    for index, (n, base, row) in enumerate(up_levels):
        for q in range(n // 2):
            value = raised(up, base + 2 + 2 * q, row + 2 * q)
            if index + 1 < len(up_levels):
                up[up_levels[index + 1][1] + 2 + q] = value
            else:
                roots[3 + d] = value

    def halo_copies(side, where):
        copies = []
        for k, (n, base, row) in enumerate(up_levels):
            src = base + 2 if side == 0 else base + n
            dst = base + 2 + n if side == 0 else base
            copies.append(
                remote(up.at[pl.ds(src, 2)], up.at[pl.ds(dst, 2)], s_h.at[side, k], r_h.at[side, k], where)
            )
        return copies

    halos_left = halo_copies(0, (jnp.maximum(d - 1, 0), v))
    halos_right = halo_copies(1, (jnp.minimum(d + 1, D - 1), v))

    @pl.when(d > 0)
    def _():
        for copy in halos_left:
            copy.start()

    @pl.when(d < D - 1)
    def _():
        for copy in halos_right:
            copy.start()

    root_copies = [
        remote(roots.at[3 + d], roots.at[3 + d], s_r.at[k], r_r.at[d], (lax.rem(d + k, D), v)) for k in range(1, D)
    ]
    for copy in root_copies:
        copy.start()

    lax.fori_loop(cut, L, near, 0)

    for s in range(D):

        @pl.when(d != s)
        def _(s=s):
            arrived(roots.at[3 + s], r_r.at[s]).wait()

    for copy in root_copies:
        copy.wait_send()

    @pl.when(d > 0)
    def _():
        for copy in halos_left:
            copy.wait_send()
        for k, (n, base, row) in enumerate(up_levels):
            arrived(up.at[pl.ds(base, 2)], r_h.at[1, k]).wait()

    @pl.when(d < D - 1)
    def _():
        for copy in halos_right:
            copy.wait_send()
        for k, (n, base, row) in enumerate(up_levels):
            arrived(up.at[pl.ds(base + 2 + n, 2)], r_h.at[0, k]).wait()

    @pl.when(has_left)
    def _():
        for copy in edges_left:
            copy.wait_send()
        for k, (n, base, row) in enumerate(local_levels):
            arrived(lev.at[pl.ds(base, 2)], r_e.at[1, k]).wait()

    @pl.when(has_right)
    def _():
        for copy in edges_right:
            copy.wait_send()
        for k, (n, base, row) in enumerate(local_levels):
            arrived(lev.at[pl.ds(base + 2 + n, 2)], r_e.at[0, k]).wait()

    top_fields = []
    for k in range(toplev):
        base, size = root_base[k], D >> k
        node = d // (1 << k)
        odd = lax.rem(node, 2).astype(F32)
        weights = (odd, 1.0, 1.0, 1.0 - odd)
        table = tops_v[k]
        partners = jnp.concatenate([coef(roots, base + 3 + node + o) for o in (-3, -2, 2, 3)], axis=0)
        moved = dot3(partners, table[:, : 4 * RK], NN)
        total = moved[:RK * 0 + NC] * weights[0]
        for j in range(1, 4):
            total = total + pltpu.roll(moved[j * NC : (j + 1) * NC], LANES - j * RK, 1) * weights[j]
        top_fields.append(total[:, :RK])
        if k + 1 < toplev:
            for q in range(size // 2):
                value = dot3(coef(roots, base + 3 + 2 * q), table[:, 4 * RK : 5 * RK], NN) + dot3(
                    coef(roots, base + 4 + 2 * q), table[:, 5 * RK :], NN
                )
                roots[root_base[k + 1] + 3 + q, :, :RK] = value
    down = top_fields[toplev - 1]
    for k in range(toplev - 2, -1, -1):
        odd = lax.rem(d // (1 << k), 2).astype(F32)
        table = tops_v[k]
        even_part = dot3(down, table[:, 4 * RK : 5 * RK], NT)
        odd_part = dot3(down, table[:, 5 * RK :], NT)
        down = top_fields[k] + even_part * (1.0 - odd) + odd_part * odd

    def coupled(ref, sources, row):
        moved = dot3(jnp.concatenate([coef(ref, i) for i in sources], axis=0), op(row), NN)
        return (
            moved[:NC]
            + pltpu.roll(moved[NC : 2 * NC], LANES - RK, 1)
            + pltpu.roll(moved[2 * NC :], LANES - 2 * RK, 1)
        )[:, :RK]

    def lowered(parent, row):
        zeros = jnp.zeros((NC, 3 * RK), F32)
        return dot3(jnp.concatenate([zeros, parent], axis=1), op(row), NT)

    for index in range(len(up_levels) - 1, -1, -1):
        n, base, row = up_levels[index]
        node = v // (V // n)
        odd = lax.rem(node, 2)
        at = base + 2 + node
        sources = (at - 2 - odd, at + 2 - 4 * odd, at + 3 - odd)
        down = coupled(up, sources, row + node) + lowered(down, row + node)
    downs = [down]
    for index in range(len(local_levels) - 1, -1, -1):
        n, base, row = local_levels[index]
        fresh = []
        for i in range(n):
            shifts = (-2, 2, 3) if i % 2 == 0 else (-3, -2, 2)
            sources = [base + 2 + i + o for o in shifts]
            where = row + v * n + i
            fresh.append(coupled(lev, sources, where) + lowered(downs[i // 2], where))
        downs = fresh

    inner = jnp.zeros((NC, NC), F32)
    for l in range(L):
        points = slice(l * PTS, (l + 1) * PTS)
        mine = win[:, H + l * PTS : H + (l + 1) * PTS]
        value = prod[:, points] + dot3(downs[l], basis_v[:, points], NN) + NUGGET * mine
        prod[:, points] = value
        inner = inner + dot3(value, mine, NT)
    for t in range(V):
        gsend[t, :, :NC] = inner[t * cols : (t + 1) * cols]

    def home(t):
        return remote(
            prod.at[pl.ds(t * cols, cols), :], out.at[:, chunk], s_o.at[t], r_o.at[v], (d, t)
        )

    def inner_copy(t):
        return remote(gsend.at[t], gpart.at[v], s_g.at[t], r_g.at[v], (d, t))

    for t in range(V):

        @pl.when(v != t)
        def _(t=t):
            inner_copy(t).start()

    stay = pltpu.make_async_copy(prod.at[own, :], out.at[:, chunk], s_loc.at[9])
    stay.start()
    for t in range(V):

        @pl.when(v != t)
        def _(t=t):
            home(t).start()

    gpart[v] = gsend[v]
    for s in range(V):

        @pl.when(v != s)
        def _(s=s):
            arrived(gpart.at[s], r_g.at[s]).wait()

    group = gpart[0]
    for s in range(1, V):
        group = group + gpart[s]
    gall[d] = group
    group_copies = [
        remote(gall.at[d], gall.at[d], s_q.at[k], r_q.at[d], (lax.rem(d + k, D), v)) for k in range(1, D)
    ]
    for copy in group_copies:
        copy.start()
    stay.wait()

    for t in range(V):

        @pl.when(v != t)
        def _(t=t):
            for copy in vec_copies(t):
                copy.wait_send()
            home(t).wait_send()
            inner_copy(t).wait_send()
            arrived(out.at[:, pl.ds(t * C, C)], r_o.at[t]).wait()

    @pl.when(d < D - 1)
    def _():
        cross_right.wait_send()

        @pl.when(v == V - 1)
        def _():
            crd_right.wait_send()

    @pl.when(d > 0)
    def _():
        cross_left.wait_send()

        @pl.when(v == 0)
        def _():
            crd_left.wait_send()

    for s in range(D):

        @pl.when(d != s)
        def _(s=s):
            arrived(gall.at[s], r_q.at[s]).wait()

    for copy in group_copies:
        copy.wait_send()
    whole = gall[0]
    for s in range(1, D):
        whole = whole + gall[s]
    gram[...] = whole * (1.0 / (D * PD))


def on_device(D, V, vectors, coords, leaf_basis, node_ops, top_ops, near_target, near_source, near_count):
    cols, points = vectors.shape
    rank = leaf_basis.shape[0]
    LD = points // PTS
    L = LD // V
    NC = cols * V
    C, H = L * PTS, REACH * PTS
    slots = near_target.shape[0]
    rounds = slots // LD
    toplev = top_ops.shape[0]
    base_leaf = lax.axis_index("leaf") * LD
    live = (jnp.arange(slots, dtype=jnp.int32) < near_count[0]).reshape(rounds, LD, 1)
    local = (near_target - base_leaf).reshape(rounds, LD, 1)
    shift = (near_source - near_target).reshape(rounds, LD, 1)
    hit = (local == jnp.arange(LD, dtype=jnp.int32)) & live
    offs = jnp.sum(jnp.where(hit, shift, 0), axis=1) + jnp.arange(LD, dtype=jnp.int32) % L + REACH
    offs = jnp.clip(offs, 0, L + 2 * REACH - 1).reshape(-1)
    wts = jnp.sum(jnp.where(hit, SIGNAL, 0.0).astype(F32), axis=1).reshape(-1)
    coords8 = jnp.pad(coords, ((0, 5), (0, 0)))

    def total(n):
        size = 0
        while n >= 2:
            size += n + 4
            n //= 2
        return size

    def depth(n):
        return max(1, n.bit_length() - 1)

    root_nodes = sum((D >> k) + 6 for k in range(toplev))
    dma = pltpu.SemaphoreType.DMA
    vmem = pltpu.VMEM
    scratch = [
        vmem((NC, C + 2 * H), F32),
        vmem((L + 2 * REACH, 2 * NC, PTS), BF16),
        vmem((8, C + 2 * H), F32),
        vmem((L + 2 * REACH, 3, PTS, LANES), F32),
        vmem((rank, C), F32),
        vmem(node_ops.shape, F32),
        vmem(top_ops.shape, F32),
        vmem((rounds, PTS, PTS), BF16),
        vmem((rounds, PTS, PTS), BF16),
        vmem((NC, C), F32),
        vmem((total(L), NC, LANES), F32),
        vmem((total(V), NC, LANES), F32),
        vmem((root_nodes, NC, LANES), F32),
        vmem((8, LANES), F32),
        vmem((V, cols, LANES), F32),
        vmem((V, cols, LANES), F32),
        vmem((D, cols, LANES), F32),
        dma((10,)),
        dma((3, V)),
        dma((3, V)),
        dma((2,)),
        dma((2, V)),
        dma((2,)),
        dma((2,)),
        dma((2, depth(L))),
        dma((2, depth(L))),
        dma((V,)),
        dma((V,)),
        dma((2, depth(V))),
        dma((2, depth(V))),
        dma((D,)),
        dma((D,)),
        dma((V,)),
        dma((V,)),
        dma((V,)),
        dma((V,)),
        dma((D,)),
        dma((D,)),
    ]
    smem = pl.BlockSpec(memory_space=pltpu.SMEM)
    anyw = pl.BlockSpec(memory_space=pl.ANY)
    product, gram = pl.pallas_call(
        functools.partial(kernel, (D, V, LD, rank, rounds, toplev)),
        out_shape=(
            jax.ShapeDtypeStruct((cols, points), F32),
            jax.ShapeDtypeStruct((cols, LANES), F32),
        ),
        in_specs=[smem, smem, anyw, anyw, anyw, anyw, anyw],
        out_specs=(anyw, pl.BlockSpec(memory_space=pltpu.VMEM)),
        scratch_shapes=scratch,
        compiler_params=pltpu.CompilerParams(
            collective_id=0, has_side_effects=True, vmem_limit_bytes=67043328
        ),
        name="hmatrix",
    )(offs, wts, vectors, coords8, leaf_basis, node_ops, top_ops)
    return product, gram[:, :NC].T


def solution(mesh):
    return jax.shard_map(
        functools.partial(on_device, mesh.shape["leaf"], mesh.shape["vec"]),
        mesh=mesh,
        in_specs=(
            P("vec", "leaf"),
            P(None, "leaf"),
            P(None, "leaf"),
            P("leaf", None, None),
            P(),
            P("leaf"),
            P("leaf"),
            P("leaf"),
        ),
        out_specs=(P("vec", "leaf"), P(None, "vec")),
        check_vma=False,
    )
```

```python
import functools

import jax
import jax.numpy as jnp
from jax import lax
from jax.experimental import pallas as pl
from jax.experimental.pallas import tpu as pltpu
from jax.sharding import PartitionSpec as P

PTS = 256
REACH = 4
SIGNAL = 0.1
NUGGET = 0.5
LENGTH = 0.35
SLAB = 0.25
SCALE = 3.0 ** 0.5 / LENGTH
MESH = pl.DeviceIdType.MESH
F32 = jnp.float32
BF16 = jnp.bfloat16
LANES = 128


def halves(x):
    high = x.astype(BF16)
    return high, (x - high.astype(F32)).astype(BF16)


def dot3(a, b, dims):
    ah, al = halves(a)
    bh, bl = halves(b)

    def one(x, y):
        return lax.dot_general(x, y, (dims, ((), ())), preferred_element_type=F32)

    return one(ah, bh) + (one(al, bh) + one(ah, bl))


NN = ((1,), (0,))
NT = ((1,), (1,))


def kernel(cfg, offs, wts, vecs, coords, basis, ops, tops, out, gram, *scr):
    D, V, LD, RK, rounds, toplev = cfg
    cols = vecs.shape[0]
    NC = cols * V
    L = LD // V
    C = L * PTS
    H = REACH * PTS
    PD = LD * PTS
    (win, vhl, crd, bcol, basis_v, ops_v, tops_v, kh, kl, prod, lev, up, roots, fld, gsend, gpart, gall) = scr[:17]
    (s_loc, s_vec, r_vec, s_x, r_x, s_c, r_c, s_e, r_e, s_u, r_u, s_h, r_h, s_r, r_r, s_o, r_o, s_g, r_g, s_q, r_q) = scr[17:]
    d = lax.axis_index("leaf")
    v = lax.axis_index("vec")
    g = d * V + v
    has_left = g > 0
    has_right = g < D * V - 1

    local_levels = []
    n, base, row = L, 0, 0
    while n >= 2:
        local_levels.append((n, base, row))
        base += n + 4
        row += LD // L * n
        n //= 2
    up_levels = []
    n, base = V, 0
    while n >= 2:
        up_levels.append((n, base, row))
        base += n + 4
        row += n
        n //= 2

    own = pl.ds(v * cols, cols)
    chunk = pl.ds(pl.multiple_of(v * C, C), C)
    loads = [
        pltpu.make_async_copy(vecs.at[:, chunk], win.at[own, pl.ds(H, C)], s_loc.at[0]),
        pltpu.make_async_copy(coords.at[:, chunk], crd.at[:, pl.ds(H, C)], s_loc.at[1]),
        pltpu.make_async_copy(basis.at[:, chunk], basis_v, s_loc.at[2]),
        pltpu.make_async_copy(ops, ops_v, s_loc.at[3]),
        pltpu.make_async_copy(tops, tops_v, s_loc.at[4]),
    ]
    for copy in loads:
        copy.start()
    low_from = pl.ds(pl.multiple_of(jnp.maximum(v * C - H, 0), H), H)
    high_from = pl.ds(pl.multiple_of(jnp.minimum(v * C + C, PD - H), H), H)
    low_loads = [
        pltpu.make_async_copy(vecs.at[:, low_from], win.at[own, pl.ds(0, H)], s_loc.at[5]),
        pltpu.make_async_copy(coords.at[:, low_from], crd.at[:, pl.ds(0, H)], s_loc.at[6]),
    ]
    high_loads = [
        pltpu.make_async_copy(vecs.at[:, high_from], win.at[own, pl.ds(H + C, H)], s_loc.at[7]),
        pltpu.make_async_copy(coords.at[:, high_from], crd.at[:, pl.ds(H + C, H)], s_loc.at[8]),
    ]

    @pl.when(v > 0)
    def _():
        for copy in low_loads:
            copy.start()

    @pl.when(v < V - 1)
    def _():
        for copy in high_loads:
            copy.start()

    barrier = pltpu.get_barrier_semaphore()
    for k in range(1, V):
        pl.semaphore_signal(barrier, inc=1, device_id=(d, lax.rem(v + k, V)), device_id_type=MESH)
    for k in range(1, D):
        pl.semaphore_signal(barrier, inc=1, device_id=(lax.rem(d + k, D), v), device_id_type=MESH)

    @pl.when(d > 0)
    def _():
        for k in range(1, V):
            pl.semaphore_signal(barrier, inc=1, device_id=(d - 1, lax.rem(v + k, V)), device_id_type=MESH)

    @pl.when(d < D - 1)
    def _():
        for k in range(1, V):
            pl.semaphore_signal(barrier, inc=1, device_id=(d + 1, lax.rem(v + k, V)), device_id_type=MESH)

    sides = (d > 0).astype(jnp.int32) + (d < D - 1).astype(jnp.int32)
    pl.semaphore_wait(barrier, V - 1 + D - 1 + (V - 1) * sides)

    def remote(src, dst, ss, rs, where):
        return pltpu.make_async_remote_copy(
            src_ref=src, dst_ref=dst, send_sem=ss, recv_sem=rs, device_id=where, device_id_type=MESH
        )

    def vec_copies(t):
        parts = [(0, t * C, H, C)]
        if t > 0:
            parts.append((1, t * C - H, 0, H))
        if t < V - 1:
            parts.append((2, t * C + C, H + C, H))
        return [
            remote(
                vecs.at[:, pl.ds(src, size)],
                win.at[own, pl.ds(dst, size)],
                s_vec.at[k, t],
                r_vec.at[k, v],
                (d, t),
            )
            for k, src, dst, size in parts
        ]

    cross_right = remote(
        vecs.at[:, pl.ds(PD - H, H)], win.at[own, pl.ds(0, H)], s_x.at[0], r_x.at[0, v], (jnp.minimum(d + 1, D - 1), 0)
    )
    cross_left = remote(
        vecs.at[:, pl.ds(0, H)], win.at[own, pl.ds(H + C, H)], s_x.at[1], r_x.at[1, v], (jnp.maximum(d - 1, 0), V - 1)
    )
    crd_right = remote(
        coords.at[:, pl.ds(PD - H, H)], crd.at[:, pl.ds(0, H)], s_c.at[0], r_c.at[0], (jnp.minimum(d + 1, D - 1), 0)
    )
    crd_left = remote(
        coords.at[:, pl.ds(0, H)], crd.at[:, pl.ds(H + C, H)], s_c.at[1], r_c.at[1], (jnp.maximum(d - 1, 0), V - 1)
    )
    for t in range(V):

        @pl.when(v != t)
        def _(t=t):
            for copy in vec_copies(t):
                copy.start()

    @pl.when(d < D - 1)
    def _():
        cross_right.start()

        @pl.when(v == V - 1)
        def _():
            crd_right.start()

    @pl.when(d > 0)
    def _():
        cross_left.start()

        @pl.when(v == 0)
        def _():
            crd_left.start()

    def zero_nodes(ref, lo, size):
        ref[lo : lo + size] = jnp.zeros((size,) + ref.shape[1:], F32)

    @pl.when(jnp.logical_not(has_left))
    def _():
        win[:, 0:H] = jnp.zeros((NC, H), F32)
        crd[:, 0:H] = jnp.zeros((crd.shape[0], H), F32)
        for n, base, row in local_levels:
            zero_nodes(lev, base, 2)

    @pl.when(jnp.logical_not(has_right))
    def _():
        win[:, H + C :] = jnp.zeros((NC, H), F32)
        crd[:, H + C :] = jnp.zeros((crd.shape[0], H), F32)
        for n, base, row in local_levels:
            zero_nodes(lev, base + 2 + n, 2)

    @pl.when(d == 0)
    def _():
        for n, base, row in up_levels:
            zero_nodes(up, base, 2)

    @pl.when(d == D - 1)
    def _():
        for n, base, row in up_levels:
            zero_nodes(up, base + 2 + n, 2)

    root_base = []
    base = 0
    for k in range(toplev):
        size = D >> k
        zero_nodes(roots, base, 3)
        zero_nodes(roots, base + 3 + size, 3)
        root_base.append(base)
        base += size + 6

    def arrived(dst, rs):
        return pltpu.make_async_copy(dst, dst, rs)

    for copy in loads:
        copy.wait()

    @pl.when(v > 0)
    def _():
        for copy in low_loads:
            copy.wait()

    @pl.when(v < V - 1)
    def _():
        for copy in high_loads:
            copy.wait()

    origin = (g * L).astype(F32) * SLAB

    def scale_points(lo, size):
        points = crd[:, lo : lo + size]
        first = lax.broadcasted_iota(jnp.int32, points.shape, 0) == 0
        crd[:, lo : lo + size] = (points - jnp.where(first, origin, 0.0)) * SCALE

    def spread_leaves(lo, count):
        pack = 4

        def spread(i, carry):
            for j in range(pack):
                leaf = lo + i * pack + j
                for half in range(PTS // LANES):
                    at = pl.ds(pl.multiple_of(leaf * PTS + half * LANES, LANES), LANES)
                    tall = crd[:, at].T
                    for axis in range(3):
                        bcol[leaf, axis, half * LANES : (half + 1) * LANES, :] = jnp.broadcast_to(
                            tall[:, axis : axis + 1], (LANES, LANES)
                        )
            return carry

        lax.fori_loop(0, count // pack, spread, 0)

    scale_points(H, C)
    spread_leaves(REACH, L)

    for s in range(V):
        rows = pl.ds(s * cols, cols)

        @pl.when(v != s)
        def _(s=s, rows=rows):
            arrived(win.at[rows, pl.ds(H, C)], r_vec.at[0, s]).wait()

    def op(i):
        return ops_v[i]

    def coef(ref, i):
        return ref[i][:, :RK]

    def raised(ref, i, row):
        both = dot3(coef(ref, i), op(row), NN) + dot3(coef(ref, i + 1), op(row + 1), NN)
        return pltpu.roll(both, RK, 1)

    for l in range(L):
        points = slice(l * PTS, (l + 1) * PTS)
        lev[2 + l, :, :RK] = dot3(win[:, H + l * PTS : H + (l + 1) * PTS], basis_v[:, points], NT)
    for index, (n, base, row) in enumerate(local_levels):
        for q in range(n // 2):
            value = raised(lev, base + 2 + 2 * q, row + v * n + 2 * q)
            if index + 1 < len(local_levels):
                lev[local_levels[index + 1][1] + 2 + q] = value
            else:
                up[2 + v] = value

    def edge_copies(side, where):
        copies = []
        for k, (n, base, row) in enumerate(local_levels):
            src = base + 2 if side == 0 else base + n
            dst = base + 2 + n if side == 0 else base
            copies.append(
                remote(lev.at[pl.ds(src, 2)], lev.at[pl.ds(dst, 2)], s_e.at[side, k], r_e.at[side, k], where)
            )
        return copies

    left_id = (jnp.maximum(g - 1, 0) // V, lax.rem(jnp.maximum(g - 1, 0), V))
    right_id = (jnp.minimum(g + 1, D * V - 1) // V, lax.rem(jnp.minimum(g + 1, D * V - 1), V))
    edges_left = edge_copies(0, left_id)
    edges_right = edge_copies(1, right_id)

    @pl.when(has_left)
    def _():
        for copy in edges_left:
            copy.start()

    @pl.when(has_right)
    def _():
        for copy in edges_right:
            copy.start()

    up_copies = [
        remote(up.at[2 + v], up.at[2 + v], s_u.at[k], r_u.at[v], (d, lax.rem(v + k, V))) for k in range(1, V)
    ]
    for copy in up_copies:
        copy.start()

    for s in range(V):
        rows = pl.ds(s * cols, cols)

        @pl.when(jnp.logical_and(v > 0, v != s))
        def _(s=s, rows=rows):
            arrived(win.at[rows, pl.ds(0, H)], r_vec.at[1, s]).wait()

        @pl.when(jnp.logical_and(v < V - 1, v != s))
        def _(s=s, rows=rows):
            arrived(win.at[rows, pl.ds(H + C, H)], r_vec.at[2, s]).wait()

        @pl.when(jnp.logical_and(v == 0, d > 0))
        def _(s=s, rows=rows):
            arrived(win.at[rows, pl.ds(0, H)], r_x.at[0, s]).wait()

        @pl.when(jnp.logical_and(v == V - 1, d < D - 1))
        def _(s=s, rows=rows):
            arrived(win.at[rows, pl.ds(H + C, H)], r_x.at[1, s]).wait()

    @pl.when(jnp.logical_and(v == 0, d > 0))
    def _():
        arrived(crd.at[:, pl.ds(0, H)], r_c.at[0]).wait()

    @pl.when(jnp.logical_and(v == V - 1, d < D - 1))
    def _():
        arrived(crd.at[:, pl.ds(H + C, H)], r_c.at[1]).wait()

    scale_points(0, H)
    scale_points(H + C, H)
    spread_leaves(0, REACH)
    spread_leaves(REACH + L, REACH)

    for leaf in range(L + 2 * REACH):
        high, low = halves(win[:, leaf * PTS : (leaf + 1) * PTS])
        vhl[leaf, :NC] = high
        vhl[leaf, NC:] = low

    step = 64

    def near(t, carry):
        here = pl.ds(pl.multiple_of(H + t * PTS, PTS), PTS)
        target = [crd[axis : axis + 1, here] for axis in range(3)]
        total = jnp.zeros((NC, PTS), F32)
        for r in range(rounds):
            slot = r * LD + v * L + t
            source = bcol[offs[slot]]
            for sub in range(PTS // step):
                rows = slice(sub * step, (sub + 1) * step)
                for half in range(PTS // LANES):
                    lanes = slice(half * LANES, (half + 1) * LANES)
                    dist = None
                    for axis in range(3):
                        gap = source[axis, rows] - target[axis][:, lanes]
                        dist = gap * gap if dist is None else dist + gap * gap
                    u = dist * lax.rsqrt(jnp.maximum(dist, 1e-30))
                    block = (1.0 + u) * jnp.exp(-u)
                    high, low = halves(block)
                    kh[r, rows, lanes] = high
                    kl[r, rows, lanes] = low
            moved = vhl[offs[slot]]
            both = jnp.dot(moved, kh[r], preferred_element_type=F32)
            small = jnp.dot(moved[:NC], kl[r], preferred_element_type=F32)
            total = total + ((both[:NC] + both[NC:]) + small) * wts[slot]
        prod[:, pl.ds(pl.multiple_of(t * PTS, PTS), PTS)] = total
        return carry

    cut = L // 2
    lax.fori_loop(0, cut, near, 0)

    for s in range(V):

        @pl.when(v != s)
        def _(s=s):
            arrived(up.at[2 + s], r_u.at[s]).wait()

    for copy in up_copies:
        copy.wait_send()
    for index, (n, base, row) in enumerate(up_levels):
        for q in range(n // 2):
            value = raised(up, base + 2 + 2 * q, row + 2 * q)
            if index + 1 < len(up_levels):
                up[up_levels[index + 1][1] + 2 + q] = value
            else:
                roots[3 + d] = value

    def halo_copies(side, where):
        copies = []
        for k, (n, base, row) in enumerate(up_levels):
            src = base + 2 if side == 0 else base + n
            dst = base + 2 + n if side == 0 else base
            copies.append(
                remote(up.at[pl.ds(src, 2)], up.at[pl.ds(dst, 2)], s_h.at[side, k], r_h.at[side, k], where)
            )
        return copies

    halos_left = halo_copies(0, (jnp.maximum(d - 1, 0), v))
    halos_right = halo_copies(1, (jnp.minimum(d + 1, D - 1), v))

    @pl.when(d > 0)
    def _():
        for copy in halos_left:
            copy.start()

    @pl.when(d < D - 1)
    def _():
        for copy in halos_right:
            copy.start()

    root_copies = [
        remote(roots.at[3 + d], roots.at[3 + d], s_r.at[k], r_r.at[d], (lax.rem(d + k, D), v)) for k in range(1, D)
    ]
    for copy in root_copies:
        copy.start()

    lax.fori_loop(cut, L, near, 0)

    for s in range(D):

        @pl.when(d != s)
        def _(s=s):
            arrived(roots.at[3 + s], r_r.at[s]).wait()

    for copy in root_copies:
        copy.wait_send()

    @pl.when(d > 0)
    def _():
        for copy in halos_left:
            copy.wait_send()
        for k, (n, base, row) in enumerate(up_levels):
            arrived(up.at[pl.ds(base, 2)], r_h.at[1, k]).wait()

    @pl.when(d < D - 1)
    def _():
        for copy in halos_right:
            copy.wait_send()
        for k, (n, base, row) in enumerate(up_levels):
            arrived(up.at[pl.ds(base + 2 + n, 2)], r_h.at[0, k]).wait()

    @pl.when(has_left)
    def _():
        for copy in edges_left:
            copy.wait_send()
        for k, (n, base, row) in enumerate(local_levels):
            arrived(lev.at[pl.ds(base, 2)], r_e.at[1, k]).wait()

    @pl.when(has_right)
    def _():
        for copy in edges_right:
            copy.wait_send()
        for k, (n, base, row) in enumerate(local_levels):
            arrived(lev.at[pl.ds(base + 2 + n, 2)], r_e.at[0, k]).wait()

    top_fields = []
    for k in range(toplev):
        base, size = root_base[k], D >> k
        node = d // (1 << k)
        odd = lax.rem(node, 2).astype(F32)
        weights = (odd, 1.0, 1.0, 1.0 - odd)
        table = tops_v[k]
        partners = jnp.concatenate([coef(roots, base + 3 + node + o) for o in (-3, -2, 2, 3)], axis=0)
        moved = dot3(partners, table[:, : 4 * RK], NN)
        total = moved[:RK * 0 + NC] * weights[0]
        for j in range(1, 4):
            total = total + pltpu.roll(moved[j * NC : (j + 1) * NC], LANES - j * RK, 1) * weights[j]
        top_fields.append(total[:, :RK])
        if k + 1 < toplev:
            for q in range(size // 2):
                value = dot3(coef(roots, base + 3 + 2 * q), table[:, 4 * RK : 5 * RK], NN) + dot3(
                    coef(roots, base + 4 + 2 * q), table[:, 5 * RK :], NN
                )
                roots[root_base[k + 1] + 3 + q, :, :RK] = value
    down = top_fields[toplev - 1]
    for k in range(toplev - 2, -1, -1):
        odd = lax.rem(d // (1 << k), 2).astype(F32)
        table = tops_v[k]
        even_part = dot3(down, table[:, 4 * RK : 5 * RK], NT)
        odd_part = dot3(down, table[:, 5 * RK :], NT)
        down = top_fields[k] + even_part * (1.0 - odd) + odd_part * odd

    def coupled(ref, sources, row):
        moved = dot3(jnp.concatenate([coef(ref, i) for i in sources], axis=0), op(row), NN)
        return (
            moved[:NC]
            + pltpu.roll(moved[NC : 2 * NC], LANES - RK, 1)
            + pltpu.roll(moved[2 * NC :], LANES - 2 * RK, 1)
        )[:, :RK]

    def lowered(parent, row):
        zeros = jnp.zeros((NC, 3 * RK), F32)
        return dot3(jnp.concatenate([zeros, parent], axis=1), op(row), NT)

    for index in range(len(up_levels) - 1, -1, -1):
        n, base, row = up_levels[index]
        node = v // (V // n)
        odd = lax.rem(node, 2)
        at = base + 2 + node
        sources = (at - 2 - odd, at + 2 - 4 * odd, at + 3 - odd)
        down = coupled(up, sources, row + node) + lowered(down, row + node)
    downs = [down]
    for index in range(len(local_levels) - 1, -1, -1):
        n, base, row = local_levels[index]
        fresh = []
        for i in range(n):
            shifts = (-2, 2, 3) if i % 2 == 0 else (-3, -2, 2)
            sources = [base + 2 + i + o for o in shifts]
            where = row + v * n + i
            fresh.append(coupled(lev, sources, where) + lowered(downs[i // 2], where))
        downs = fresh

    inner = jnp.zeros((NC, NC), F32)
    for l in range(L):
        points = slice(l * PTS, (l + 1) * PTS)
        mine = win[:, H + l * PTS : H + (l + 1) * PTS]
        value = prod[:, points] + dot3(downs[l], basis_v[:, points], NN) + NUGGET * mine
        prod[:, points] = value
        inner = inner + dot3(value, mine, NT)
    for t in range(V):
        gsend[t, :, :NC] = inner[t * cols : (t + 1) * cols]

    def home(t):
        return remote(
            prod.at[pl.ds(t * cols, cols), :], out.at[:, chunk], s_o.at[t], r_o.at[v], (d, t)
        )

    def inner_copy(t):
        return remote(gsend.at[t], gpart.at[v], s_g.at[t], r_g.at[v], (d, t))

    for t in range(V):

        @pl.when(v != t)
        def _(t=t):
            inner_copy(t).start()

    stay = pltpu.make_async_copy(prod.at[own, :], out.at[:, chunk], s_loc.at[9])
    stay.start()
    for t in range(V):

        @pl.when(v != t)
        def _(t=t):
            home(t).start()

    gpart[v] = gsend[v]
    for s in range(V):

        @pl.when(v != s)
        def _(s=s):
            arrived(gpart.at[s], r_g.at[s]).wait()

    group = gpart[0]
    for s in range(1, V):
        group = group + gpart[s]
    gall[d] = group
    group_copies = [
        remote(gall.at[d], gall.at[d], s_q.at[k], r_q.at[d], (lax.rem(d + k, D), v)) for k in range(1, D)
    ]
    for copy in group_copies:
        copy.start()
    stay.wait()

    for t in range(V):

        @pl.when(v != t)
        def _(t=t):
            for copy in vec_copies(t):
                copy.wait_send()
            home(t).wait_send()
            inner_copy(t).wait_send()
            arrived(out.at[:, pl.ds(t * C, C)], r_o.at[t]).wait()

    @pl.when(d < D - 1)
    def _():
        cross_right.wait_send()

        @pl.when(v == V - 1)
        def _():
            crd_right.wait_send()

    @pl.when(d > 0)
    def _():
        cross_left.wait_send()

        @pl.when(v == 0)
        def _():
            crd_left.wait_send()

    for s in range(D):

        @pl.when(d != s)
        def _(s=s):
            arrived(gall.at[s], r_q.at[s]).wait()

    for copy in group_copies:
        copy.wait_send()
    whole = gall[0]
    for s in range(1, D):
        whole = whole + gall[s]
    gram[...] = whole * (1.0 / (D * PD))


def on_device(D, V, vectors, coords, leaf_basis, node_ops, top_ops, near_target, near_source, near_count):
    cols, points = vectors.shape
    rank = leaf_basis.shape[0]
    LD = points // PTS
    L = LD // V
    NC = cols * V
    C, H = L * PTS, REACH * PTS
    slots = near_target.shape[0]
    rounds = slots // LD
    toplev = top_ops.shape[0]
    base_leaf = lax.axis_index("leaf") * LD
    live = (jnp.arange(slots, dtype=jnp.int32) < near_count[0]).reshape(rounds, LD, 1)
    local = (near_target - base_leaf).reshape(rounds, LD, 1)
    shift = (near_source - near_target).reshape(rounds, LD, 1)
    hit = (local == jnp.arange(LD, dtype=jnp.int32)) & live
    offs = jnp.sum(jnp.where(hit, shift, 0), axis=1) + jnp.arange(LD, dtype=jnp.int32) % L + REACH
    offs = jnp.clip(offs, 0, L + 2 * REACH - 1).reshape(-1)
    wts = jnp.sum(jnp.where(hit, SIGNAL, 0.0).astype(F32), axis=1).reshape(-1)

    def total(n):
        size = 0
        while n >= 2:
            size += n + 4
            n //= 2
        return size

    def depth(n):
        return max(1, n.bit_length() - 1)

    root_nodes = sum((D >> k) + 6 for k in range(toplev))
    dma = pltpu.SemaphoreType.DMA
    vmem = pltpu.VMEM
    scratch = [
        vmem((NC, C + 2 * H), F32),
        vmem((L + 2 * REACH, 2 * NC, PTS), BF16),
        vmem((3, C + 2 * H), F32),
        vmem((L + 2 * REACH, 3, PTS, LANES), F32),
        vmem((rank, C), F32),
        vmem(node_ops.shape, F32),
        vmem(top_ops.shape, F32),
        vmem((rounds, PTS, PTS), BF16),
        vmem((rounds, PTS, PTS), BF16),
        vmem((NC, C), F32),
        vmem((total(L), NC, LANES), F32),
        vmem((total(V), NC, LANES), F32),
        vmem((root_nodes, NC, LANES), F32),
        vmem((8, LANES), F32),
        vmem((V, cols, LANES), F32),
        vmem((V, cols, LANES), F32),
        vmem((D, cols, LANES), F32),
        dma((10,)),
        dma((3, V)),
        dma((3, V)),
        dma((2,)),
        dma((2, V)),
        dma((2,)),
        dma((2,)),
        dma((2, depth(L))),
        dma((2, depth(L))),
        dma((V,)),
        dma((V,)),
        dma((2, depth(V))),
        dma((2, depth(V))),
        dma((D,)),
        dma((D,)),
        dma((V,)),
        dma((V,)),
        dma((V,)),
        dma((V,)),
        dma((D,)),
        dma((D,)),
    ]
    smem = pl.BlockSpec(memory_space=pltpu.SMEM)
    anyw = pl.BlockSpec(memory_space=pl.ANY)
    product, gram = pl.pallas_call(
        functools.partial(kernel, (D, V, LD, rank, rounds, toplev)),
        out_shape=(
            jax.ShapeDtypeStruct((cols, points), F32),
            jax.ShapeDtypeStruct((cols, LANES), F32),
        ),
        in_specs=[smem, smem, anyw, anyw, anyw, anyw, anyw],
        out_specs=(anyw, pl.BlockSpec(memory_space=pltpu.VMEM)),
        scratch_shapes=scratch,
        compiler_params=pltpu.CompilerParams(
            collective_id=0, has_side_effects=True, vmem_limit_bytes=67043328
        ),
        name="hmatrix",
    )(offs, wts, vectors, coords, leaf_basis, node_ops, top_ops)
    return product, gram[:, :NC].T


def solution(mesh):
    return jax.shard_map(
        functools.partial(on_device, mesh.shape["leaf"], mesh.shape["vec"]),
        mesh=mesh,
        in_specs=(
            P("vec", "leaf"),
            P(None, "leaf"),
            P(None, "leaf"),
            P("leaf", None, None),
            P(),
            P("leaf"),
            P("leaf"),
            P("leaf"),
        ),
        out_specs=(P("vec", "leaf"), P(None, "vec")),
        check_vma=False,
    )
```
